32 devices in a mesh: dp: 8 (over y, x, core), tensor: 4 (over z).
Axes of the slice: x: 2, y: 2, z: 4, core: 2. Of those that a mesh axis runs over, the one named last changes fastest.
Arguments:
- queries: bfloat16 [256, 32, 16384], P('dp', None, 'tensor'), may hold values from -6 to 6
- key_rows: bfloat16 [256, 32, 1024], P(('dp', 'tensor')), may hold values from -6 to 6
- value_rows: bfloat16 [256, 32, 1024], P(('dp', 'tensor')), may hold values from -6 to 6
- destination: int32 [256], P('dp'), may hold values from 0 to 7, as said below
- token_count: int32 [256], P('dp'), may hold values from 16 to 32, as said below
- doc_ids: int32 [8, 1024], P('dp'), may hold values from 0 to 7, never falling along the last dimension, each value on 1 to 256 neighbouring positions
Outputs:
- attended: bfloat16 [8192, 16384], P('dp', 'tensor')
The draws below stay inside these ranges and needn't reach their ends.
Inputs may be any that keep to these rules, and one draw needn't show every extreme that they name: `destination`: every data group is named by exactly 32 sentences; of the 32 sentences of one group at most 8 name the same group, and some group sends exactly 8 sentences to one group in every draw. `token_count`: in every draw some data group receives only sentences with 32 live tokens, so its total is 1024.
All inputs are finite; a program needn't handle non-finite values.
Results may differ from the reference program's by a relative error of at most 0.0034.
Values may be sent and summed in bfloat16 or wider, within the bound.
A program may use at most 256 MiB of HBM per device.

```python
import math
import jax
import jax.numpy as jnp
import numpy as np
from jax import lax

HEADS = 128
KV_HEADS = 8
HEAD_DIM = 128
SENT = 32
SLOT = 32
ROW = 1024
CAP = 8
N_DP = 8


def draw_queries(key, part):
    shape = (N_DP * SENT, SLOT, HEADS, HEAD_DIM)
    base = jnp.clip(jax.random.normal(jax.random.fold_in(key, 34), shape, jnp.float32), -6.0, 6.0)
    return base.reshape(N_DP * SENT, SLOT, HEADS * HEAD_DIM).astype(jnp.bfloat16)


def draw_key_rows(key, part):
    shape = (N_DP * SENT, SLOT, KV_HEADS, HEAD_DIM)
    base = jnp.clip(jax.random.normal(jax.random.fold_in(key, 44), shape, jnp.float32), -6.0, 6.0)
    return base.reshape(N_DP * SENT, SLOT, KV_HEADS * HEAD_DIM).astype(jnp.bfloat16)


def draw_destination(key, part):
    sigma = jax.random.permutation(jax.random.fold_in(key, 11), N_DP)
    tau = jax.random.permutation(jax.random.fold_in(key, 12), N_DP)
    spare = jax.random.permutation(jax.random.fold_in(key, 13), jnp.arange(CAP * (N_DP - 1), dtype=jnp.int32) % (N_DP - 1)) + 1
    offsets = jnp.concatenate([jnp.zeros((CAP,), jnp.int32), spare[:SENT - CAP].astype(jnp.int32)])
    source_keys = jax.random.split(jax.random.fold_in(key, 14), N_DP)
    shuffles = jax.vmap(lambda one_key: jax.random.permutation(one_key, SENT))(source_keys)
    lanes = offsets[shuffles]
    target = sigma[(tau[:, None] + lanes) % N_DP]
    return target.reshape(N_DP * SENT).astype(jnp.int32)


def draw_token_count(key, part):
    levels = jax.random.randint(jax.random.fold_in(key, 21), (N_DP, 1), 2, 5)
    raw = jax.random.randint(jax.random.fold_in(key, 22), (N_DP, SENT), 0, SLOT // 2 + 1)
    counts = (SLOT // 2 + raw * levels // 4).reshape(N_DP * SENT)
    counts = jnp.minimum(counts, SLOT)
    routed = draw_destination(key, part)
    counts = jnp.where(routed == routed[0], SLOT, counts)
    return counts.astype(jnp.int32)


def block_scale(own_key, extent, cuts, smallest, largest):
    loudness, own = 1.0, jax.random.fold_in(own_key, 6)
    for dim, shards_of in cuts:
        heights = jnp.exp(jax.random.uniform(jax.random.fold_in(own, dim), (shards_of,), jnp.float32, smallest / len(cuts), largest / len(cuts)))
        loudness = loudness * jnp.repeat(heights, extent[dim] // shards_of).reshape([-1 if axis == dim else 1 for axis in range(len(extent))])
    return loudness


def profile(number_of, total, limit, skew):
    portions = [(1 << 20) // math.isqrt(standing ** skew) + 1 for standing in range(2, number_of + 1)]
    rest, given = total - limit - (number_of - 1), [1] * (number_of - 1)
    while rest > 0:
        candidates = [i for i in range(number_of - 1) if given[i] < limit]
        mass, budget = sum([portions[i] for i in candidates]), rest
        for i in candidates:
            extra = min(limit - given[i], max(1, budget * portions[i] // mass), rest)
            given[i] = given[i] + extra
            rest = rest - extra
    return np.array([limit] + given)


def ragged_sizes(rng, number_of, total, bound, skew):
    if number_of == 2:
        one = jax.random.randint(rng, (), max(1, total - bound), min(bound, total - 1) + 1)
        return jnp.stack([one, total - one])
    lengths = jnp.asarray(profile(number_of, total, bound, skew), jnp.int32)
    pairs = (number_of - 1) // 2
    source_of, sink = lengths[1:1 + 2 * pairs:2], lengths[2:2 + 2 * pairs:2]
    room = jnp.minimum(source_of - 1, bound - sink)
    moved = jax.random.randint(jax.random.fold_in(rng, 1), (pairs,), 0, 1 << 20) % (room + 1)
    lengths = lengths.at[1:1 + 2 * pairs:2].set(source_of - moved).at[2:2 + 2 * pairs:2].set(sink + moved)
    return lengths[jax.random.permutation(jax.random.fold_in(rng, 2), number_of)]


def centred(stream_key, dims, scale, bound, cuts=(), kind=jnp.bfloat16):
    values = scale * jax.random.normal(stream_key, dims, jnp.float32)
    if cuts:
        values = values * block_scale(stream_key, dims, cuts, -0.22, 0.18)
    return jnp.clip(values, -bound, bound).astype(kind)


def setup_inputs(seed: int = 0) -> dict:
    key_list = jax.random.split(jax.random.key(seed), 7)
    queries = draw_queries(jax.random.fold_in(key_list[6], 71), 0)
    key_rows = draw_key_rows(jax.random.fold_in(key_list[6], 71), 0)
    value_rows = centred(key_list[2], (N_DP * SENT, SLOT, KV_HEADS * HEAD_DIM), 1.0, 6.0, ((0, 32),))
    destination = draw_destination(jax.random.fold_in(key_list[6], 71), 0)
    token_count = draw_token_count(jax.random.fold_in(key_list[6], 71), 0)
    doc_ids = jax.vmap(lambda own: jnp.searchsorted(jnp.cumsum(ragged_sizes(own, 8, ROW, ROW // 4, 2)), jnp.arange(ROW), side="right"))(jax.random.split(key_list[5], N_DP)).reshape((N_DP, ROW)).astype(jnp.int32)
    return dict(queries=queries, key_rows=key_rows, value_rows=value_rows, destination=destination, token_count=token_count, doc_ids=doc_ids)


def pack_group(group, queries, key_rows, value_rows, destination, token_count):
    chosen = destination == group
    live = jnp.where(chosen, token_count, 0).astype(jnp.int32)
    ends = jnp.cumsum(live).astype(jnp.int32)
    starts = ends - live
    total = ends[-1]
    place = jnp.arange(ROW, dtype=jnp.int32)
    which = jnp.sum((place[:, None] >= ends[None, :]).astype(jnp.int32), axis=1).astype(jnp.int32)
    which = jnp.minimum(which, destination.shape[0] - 1)
    offset = jnp.clip(place - starts[which], 0, SLOT - 1).astype(jnp.int32)
    return queries[which, offset], key_rows[which, offset], value_rows[which, offset], total


def reference(queries, key_rows, value_rows, destination, token_count, doc_ids):
    group_size = HEADS // KV_HEADS
    scale_factor = HEAD_DIM ** -0.5

    def one_group(group):
        packed_q, packed_k, packed_v, total = pack_group(group, queries, key_rows, value_rows, destination, token_count)
        docs = lax.dynamic_index_in_dim(doc_ids, group, 0, keepdims=False)
        place = jnp.arange(ROW, dtype=jnp.int32)
        allowed = (place[None, :] <= place[:, None]) & (docs[None, :] == docs[:, None]) & (place[:, None] < total)
        q_heads = jnp.transpose(packed_q.reshape(ROW, HEADS, HEAD_DIM), (1, 0, 2))
        k_heads = jnp.transpose(packed_k.reshape(ROW, KV_HEADS, HEAD_DIM), (1, 0, 2))
        v_heads = jnp.transpose(packed_v.reshape(ROW, KV_HEADS, HEAD_DIM), (1, 0, 2))
        head_kv = (jnp.arange(HEADS, dtype=jnp.int32) // group_size).astype(jnp.int32)

        def one_head(item):
            q_head, kv_index = item
            k_head = lax.dynamic_index_in_dim(k_heads, kv_index, 0, keepdims=False)
            v_head = lax.dynamic_index_in_dim(v_heads, kv_index, 0, keepdims=False)
            scores = jnp.dot(q_head, k_head.T, preferred_element_type=jnp.float32) * scale_factor
            peak = jnp.max(jnp.where(allowed, scores, -1e30), axis=1, keepdims=True)
            weight = jnp.where(allowed, jnp.exp(scores - peak), 0.0)
            norm = jnp.sum(weight, axis=1, keepdims=True)
            mixed = jnp.dot(weight.astype(jnp.bfloat16), v_head, preferred_element_type=jnp.float32)
            return jnp.where(norm > 0, mixed / jnp.where(norm > 0, norm, 1.0), 0.0)

        outputs = lax.map(one_head, (q_heads, head_kv))
        return jnp.transpose(outputs, (1, 0, 2)).reshape(ROW, HEADS * HEAD_DIM).astype(jnp.bfloat16)

    result = lax.map(one_group, jnp.arange(N_DP, dtype=jnp.int32))
    return result.reshape(N_DP * ROW, HEADS * HEAD_DIM)
```

```python
import functools
import jax
import jax.numpy as jnp
from jax import lax
from jax.experimental import pallas as pl
from jax.experimental.pallas import tpu as pltpu
from jax.sharding import PartitionSpec as P

HEAD_DIM = 128
DOC_MAX = 256
LEAST = 16
TILE = 128
CHUNK_HEADS = 8
NEG = -1e30
LOG2E = 1.4426950408889634


def bucket_kernel(target_ref, rows_ref, out_ref, sem, *, col, width):
    count = target_ref.shape[0]

    for s in range(count):
        pltpu.make_async_copy(
            rows_ref.at[s, :, pl.ds(col, width)], out_ref.at[target_ref[s]], sem
        ).start()
    pltpu.make_async_copy(
        rows_ref.at[:, :, pl.ds(col, width)], out_ref.at[pl.ds(0, count)], sem
    ).wait()


def bucket(rows, target, slots, col, width):
    return pl.pallas_call(
        functools.partial(bucket_kernel, col=col, width=width),
        grid_spec=pltpu.PrefetchScalarGridSpec(
            num_scalar_prefetch=1,
            grid=(1,),
            in_specs=[pl.BlockSpec(memory_space=pl.ANY)],
            out_specs=pl.BlockSpec(memory_space=pl.ANY),
            scratch_shapes=[pltpu.SemaphoreType.DMA],
        ),
        out_shape=jax.ShapeDtypeStruct((slots, rows.shape[1], width), rows.dtype),
        cost_estimate=pl.CostEstimate(
            flops=0, transcendentals=0, bytes_accessed=4 * rows.shape[0] * rows.shape[1] * width
        ),
        name="bucket",
    )(target, rows)


def attend_kernel(
    slot_ref, first_ref, q_ref, kv_ref, pick_ref, bias_ref, *rest, kv_head, kv_width, heads, span
):
    out_ref, q_buf, kv_buf, k_pad, v_pad, sem_q, sem_kv = rest[-7:]
    tile = pl.program_id(0)
    sentences, slot_len, window = slot_ref.shape[0], q_ref.shape[1], pick_ref.shape[1]
    tiles = pl.num_programs(0)

    @pl.when(tile == 0)
    def _():
        for k in range(sentences):
            slot = slot_ref[k]
            rows = pl.ds(k * slot_len, slot_len)
            pltpu.make_async_copy(kv_ref.at[slot], kv_buf.at[rows], sem_kv).start()
            pltpu.make_async_copy(q_ref.at[slot], q_buf.at[rows], sem_q).start()
        pltpu.make_async_copy(kv_buf, kv_buf, sem_kv).wait()
        k_pad[:DOC_MAX] = jnp.zeros((DOC_MAX, HEAD_DIM), jnp.bfloat16)
        v_pad[:DOC_MAX] = jnp.zeros((DOC_MAX, HEAD_DIM), jnp.bfloat16)

        @pl.loop(0, tiles)
        def _(t):
            begin = pl.multiple_of(first_ref[t] * slot_len, slot_len)
            here = pl.multiple_of(t * TILE, TILE)
            pick = pick_ref[pl.ds(here, TILE), :]
            for pad, col in ((k_pad, kv_head * HEAD_DIM), (v_pad, kv_width + kv_head * HEAD_DIM)):
                piece = kv_buf[pl.ds(begin, window), col : col + HEAD_DIM]
                pad[pl.ds(DOC_MAX + here, TILE), :] = jnp.dot(
                    pick, piece, preferred_element_type=jnp.float32
                ).astype(jnp.bfloat16)

        pltpu.make_async_copy(q_buf, q_buf, sem_q).wait()

    here = pl.multiple_of(tile * TILE, TILE)
    begin = pl.multiple_of(first_ref[tile] * slot_len, slot_len)
    pick = pick_ref[pl.ds(here, TILE), :]
    bias = bias_ref[pl.ds(here, TILE), :]
    live = jnp.max(bias, axis=1, keepdims=True) > -1.0
    keys = k_pad[pl.ds(here, span), :]
    values = v_pad[pl.ds(here, span), :]
    scale = (HEAD_DIM**-0.5) * LOG2E
    for h in range(heads):
        cols = slice(h * HEAD_DIM, (h + 1) * HEAD_DIM)
        q = jnp.dot(
            pick, q_buf[pl.ds(begin, window), cols], preferred_element_type=jnp.float32
        ).astype(jnp.bfloat16)
        score = lax.dot_general(
            q, keys, (((1,), (1,)), ((), ())), preferred_element_type=jnp.float32
        )
        score = score * scale + bias
        peak = jnp.max(score, axis=1, keepdims=True)
        weight = jnp.exp2(score - peak)
        norm = jnp.sum(weight, axis=1, keepdims=True)
        mixed = jnp.dot(weight.astype(jnp.bfloat16), values, preferred_element_type=jnp.float32)
        out_ref[:, cols] = jnp.where(live, mixed / norm, 0.0).astype(jnp.bfloat16)


def attend(slot, first, q, kv, pick, bias, out, chunk, heads, kv_head, row_len, width):
    sentences, slot_len = slot.shape[0], q.shape[1]
    kv_width = kv.shape[2] // 2
    span = DOC_MAX + TILE
    chunk_width = heads * HEAD_DIM
    whole = pl.BlockSpec(memory_space=pltpu.VMEM)
    anywhere = pl.BlockSpec(memory_space=pl.ANY)
    operands = [slot, first, q, kv, pick, bias]
    specs = [anywhere, anywhere, whole, whole]
    aliases = {}
    if out is not None:
        operands.append(out)
        specs.append(anywhere)
        aliases = {6: 0}
    return pl.pallas_call(
        functools.partial(
            attend_kernel, kv_head=kv_head, kv_width=kv_width, heads=heads, span=span
        ),
        grid_spec=pltpu.PrefetchScalarGridSpec(
            num_scalar_prefetch=2,
            grid=(row_len // TILE,),
            in_specs=specs,
            out_specs=pl.BlockSpec((TILE, chunk_width), lambda t, *_: (t, chunk)),
            scratch_shapes=[
                pltpu.VMEM((sentences * slot_len, chunk_width), jnp.bfloat16),
                pltpu.VMEM((sentences * slot_len, 2 * kv_width), jnp.bfloat16),
                pltpu.VMEM((DOC_MAX + row_len, HEAD_DIM), jnp.bfloat16),
                pltpu.VMEM((DOC_MAX + row_len, HEAD_DIM), jnp.bfloat16),
                pltpu.SemaphoreType.DMA,
                pltpu.SemaphoreType.DMA,
            ],
        ),
        out_shape=jax.ShapeDtypeStruct((row_len, width), jnp.bfloat16),
        input_output_aliases=aliases,
        compiler_params=pltpu.CompilerParams(vmem_limit_bytes=32 << 20),
        cost_estimate=pl.CostEstimate(
            flops=4 * row_len * span * chunk_width,
            transcendentals=row_len * span * heads,
            bytes_accessed=6 * row_len * chunk_width,
        ),
        name="attend",
    )(*operands)


def per_device(queries, key_rows, value_rows, destination, token_count, doc_ids):
    groups = lax.axis_size("dp")
    ways = lax.axis_size("tensor")
    own_group = lax.axis_index("dp")
    sentences = destination.shape[0]
    slot_len = queries.shape[1]
    capacity = max(2, (2 * sentences + groups - 1) // groups)
    slots = groups * capacity
    row_len = doc_ids.shape[1]
    q_width = queries.shape[2]
    kv_width = key_rows.shape[2] // ways
    per_group = q_width // kv_width
    heads = min(CHUNK_HEADS, per_group)
    chunk_width = heads * HEAD_DIM

    def split(rows):
        return rows.reshape(rows.shape[0], slot_len, ways, kv_width)

    kv = jnp.concatenate([split(key_rows), split(value_rows)], axis=3)
    kv = lax.all_to_all(
        jnp.transpose(kv, (2, 0, 1, 3)), "tensor", split_axis=0, concat_axis=0, tiled=True
    ).reshape(sentences, slot_len, 2 * kv_width)

    order = jnp.arange(sentences, dtype=jnp.int32)
    same_dest = destination[:, None] == destination[None, :]
    earlier = order[None, :] < order[:, None]
    rank_in = jnp.sum((same_dest & earlier).astype(jnp.int32), axis=1)
    target = destination * capacity + rank_in

    def exchange(rows, col, width):
        return lax.all_to_all(
            bucket(rows, target, slots, col, width), "dp", split_axis=0, concat_axis=0, tiled=True
        )

    both = jnp.stack([destination, token_count])
    table = lax.all_gather(both, "dp", axis=0)
    mine = table[:, 0, :] == own_group
    place_rank = jnp.cumsum(mine.astype(jnp.int32), axis=1) - 1
    slot_ids = jnp.arange(capacity, dtype=jnp.int32)
    hits = mine[:, :, None] & (place_rank[:, :, None] == slot_ids[None, None, :])
    sizes = jnp.sum(jnp.where(hits, table[:, 1, :, None], 0), axis=1).reshape(slots)
    filled = sizes > 0
    nth = jnp.cumsum(filled.astype(jnp.int32)) - 1
    is_nth = filled[None, :] & (nth[None, :] == order[:, None])
    slot_of = jnp.sum(jnp.where(is_nth, jnp.arange(slots, dtype=jnp.int32)[None, :], 0), axis=1)
    count_of = jnp.sum(jnp.where(is_nth, sizes[None, :], 0), axis=1)
    ends = jnp.cumsum(count_of)
    total = ends[-1]
    place = jnp.arange(row_len, dtype=jnp.int32)
    passed = place[:, None] >= ends[None, :]
    which = jnp.sum(passed.astype(jnp.int32), axis=1)
    start = jnp.sum(jnp.where(passed, count_of[None, :], 0), axis=1)
    live = place < total
    flat = jnp.where(live, which * slot_len + place - start, -1)
    spread = min(sentences, (TILE - 1 + LEAST - 1) // LEAST + 1)
    first = jnp.minimum(which.reshape(-1, TILE)[:, 0], sentences - spread)
    window = spread * slot_len
    relative = flat - jnp.repeat(first, TILE) * slot_len
    pick = (
        live[:, None] & (relative[:, None] == jnp.arange(window, dtype=jnp.int32)[None, :])
    ).astype(jnp.bfloat16)
    span = DOC_MAX + TILE
    padded = jnp.concatenate([jnp.full((DOC_MAX,), -1, jnp.int32), doc_ids[0]])
    tiles = row_len // TILE
    key_docs = jnp.stack([padded[t * TILE : t * TILE + span] for t in range(tiles)])
    col = jnp.arange(span, dtype=jnp.int32)[None, None, :]
    row = jnp.arange(TILE, dtype=jnp.int32)[None, :, None]
    allowed = (
        (col - DOC_MAX <= row)
        & (key_docs[:, None, :] == doc_ids[0].reshape(tiles, TILE)[:, :, None])
        & live.reshape(tiles, TILE)[:, :, None]
    )
    bias = jnp.where(allowed, 0.0, NEG).astype(jnp.float32).reshape(row_len, span)

    got_kv = exchange(kv, 0, 2 * kv_width)
    out = None
    for chunk in range(q_width // chunk_width):
        got_q = exchange(queries, chunk * chunk_width, chunk_width)
        kv_head = chunk * heads // per_group
        out = attend(
            slot_of, first, got_q, got_kv, pick, bias, out, chunk, heads, kv_head, row_len, q_width
        )
    return out


def solution(mesh):
    placed = (
        P("dp", None, "tensor"),
        P(("dp", "tensor"), None, None),
        P(("dp", "tensor"), None, None),
        P("dp"),
        P("dp"),
        P("dp", None),
    )
    return jax.shard_map(
        per_device, mesh=mesh, in_specs=placed, out_specs=P("dp", "tensor"), check_vma=False
    )
```

```python
import functools
import jax
import jax.numpy as jnp
from jax import lax
from jax.experimental import pallas as pl
from jax.experimental.pallas import tpu as pltpu
from jax.sharding import PartitionSpec as P

HEAD_DIM = 128
DOC_MAX = 256
LEAST = 16
TILE = 128
CHUNK_HEADS = 8
STACK = 4
NEG = -1e30
LOG2E = 1.4426950408889634
WHOLE = pl.BlockSpec(memory_space=pltpu.VMEM)
ANYWHERE = pl.BlockSpec(memory_space=pl.ANY)


def fetch(code_ref, sources, cols, bases, buf, sem):
    def one(k, carry):
        code = code_ref[k]
        for i, (source, col) in enumerate(zip(sources, cols)):

            def start(i=i, source=source, col=col):
                pltpu.make_async_copy(
                    source.at[code - bases[i], :, pl.ds(col, buf.shape[2])], buf.at[k], sem
                ).start()

            if len(sources) == 1:
                start()
            else:
                inside = code >= bases[i]
                if i + 1 < len(sources):
                    inside = inside & (code < bases[i + 1])
                pl.when(inside)(start)
        return carry

    lax.fori_loop(0, buf.shape[0], one, 0, unroll=4 if buf.shape[0] % 4 == 0 else 1)


def gather_kernel(code_ref, *rest, cols, bases):
    *sources, out_ref, sem = rest
    fetch(code_ref, sources, cols, bases, out_ref, sem)
    pltpu.make_async_copy(out_ref, out_ref, sem).wait()


def gather(codes, sources, cols, bases, width):
    slot_len = sources[0].shape[1]
    shape = (codes.shape[0], slot_len, width)
    return pl.pallas_call(
        functools.partial(gather_kernel, cols=cols, bases=bases),
        grid_spec=pltpu.PrefetchScalarGridSpec(
            num_scalar_prefetch=1,
            grid=(1,),
            in_specs=[ANYWHERE] * len(sources),
            out_specs=pl.BlockSpec(shape, lambda i, *_: (0, 0, 0)),
            scratch_shapes=[pltpu.SemaphoreType.DMA],
        ),
        out_shape=jax.ShapeDtypeStruct(shape, sources[0].dtype),
        compiler_params=pltpu.CompilerParams(vmem_limit_bytes=16 << 20),
        cost_estimate=pl.CostEstimate(
            flops=0, transcendentals=0, bytes_accessed=4 * shape[0] * slot_len * width
        ),
        name="gather",
    )(codes, *sources)


def pack_kernel(code_ref, first_ref, pick_ref, *rest, cols, bases):
    *sources, k_ref, v_ref, buf, sem = rest
    kv_local, slot_len, window = k_ref.shape[0], buf.shape[1], pick_ref.shape[1]
    fetch(code_ref, sources, cols, bases, buf, sem)
    pltpu.make_async_copy(buf, buf, sem).wait()
    for ref in (k_ref, v_ref):
        ref[:, :DOC_MAX, :] = jnp.zeros((kv_local, DOC_MAX, HEAD_DIM), jnp.bfloat16)

    @pl.loop(0, pick_ref.shape[0] // TILE)
    def _(t):
        here = pl.multiple_of(t * TILE, TILE)
        rows = buf[pl.ds(first_ref[t], window // slot_len)].reshape(window, buf.shape[2])
        packed = jnp.dot(
            pick_ref[pl.ds(here, TILE), :], rows, preferred_element_type=jnp.float32
        ).astype(jnp.bfloat16)
        for n in range(2 * kv_local):
            ref = (k_ref, v_ref)[n // kv_local]
            ref[n % kv_local, pl.ds(DOC_MAX + here, TILE), :] = packed[
                :, n * HEAD_DIM : (n + 1) * HEAD_DIM
            ]


def pack(codes, first, pick, sources, cols, bases, kv_local):
    slot_len = sources[0].shape[1]
    shape = jax.ShapeDtypeStruct((kv_local, DOC_MAX + pick.shape[0], HEAD_DIM), jnp.bfloat16)
    return pl.pallas_call(
        functools.partial(pack_kernel, cols=cols, bases=bases),
        grid_spec=pltpu.PrefetchScalarGridSpec(
            num_scalar_prefetch=2,
            grid=(1,),
            in_specs=[WHOLE] + [ANYWHERE] * len(sources),
            out_specs=[WHOLE, WHOLE],
            scratch_shapes=[
                pltpu.VMEM((codes.shape[0], slot_len, 2 * kv_local * HEAD_DIM), jnp.bfloat16),
                pltpu.SemaphoreType.DMA,
            ],
        ),
        out_shape=[shape, shape],
        compiler_params=pltpu.CompilerParams(vmem_limit_bytes=16 << 20),
        name="pack",
    )(codes, first, pick, *sources)


def attend_kernel(code_ref, first_ref, k_ref, v_ref, pick_ref, bias_ref, *rest, cols, bases, heads):
    *sources, out_ref, q_buf, q_rows, sem = rest
    sources = sources[: len(cols)]
    tile = pl.program_id(0)
    slot_len, window = q_buf.shape[1], pick_ref.shape[1]
    span = bias_ref.shape[1]

    @pl.when(tile == 0)
    def _():
        fetch(code_ref, sources, cols, bases, q_buf, sem)
        pltpu.make_async_copy(q_buf, q_buf, sem).wait()

    here = pl.multiple_of(tile * TILE, TILE)
    pick = pick_ref[pl.ds(here, TILE), :]
    bias = bias_ref[pl.ds(here, TILE), :]
    live = jnp.max(bias, axis=1, keepdims=True) > -1.0
    keys = k_ref[pl.ds(here, span), :]
    values = v_ref[pl.ds(here, span), :]
    rows = q_buf[pl.ds(first_ref[tile], window // slot_len)].reshape(window, q_buf.shape[2])
    packed = jnp.dot(pick, rows, preferred_element_type=jnp.float32).astype(jnp.bfloat16)
    for h in range(heads):
        q_rows[h * TILE : (h + 1) * TILE, :] = packed[:, h * HEAD_DIM : (h + 1) * HEAD_DIM]
    scale = (HEAD_DIM**-0.5) * LOG2E
    stack = min(STACK, heads)
    for g in range(heads // stack):
        score = lax.dot_general(
            q_rows[g * stack * TILE : (g + 1) * stack * TILE, :],
            keys,
            (((1,), (1,)), ((), ())),
            preferred_element_type=jnp.float32,
        ).reshape(stack, TILE, span)
        score = score * scale + bias[None]
        peak = jnp.max(score, axis=2, keepdims=True)
        weight = jnp.exp2(score - peak)
        norm = jnp.sum(weight, axis=2, keepdims=True)
        mixed = jnp.dot(
            weight.astype(jnp.bfloat16).reshape(stack * TILE, span),
            values,
            preferred_element_type=jnp.float32,
        ).reshape(stack, TILE, HEAD_DIM)
        result = jnp.where(live[None], mixed / norm, 0.0).astype(jnp.bfloat16)
        for n in range(stack):
            h = g * stack + n
            out_ref[:, h * HEAD_DIM : (h + 1) * HEAD_DIM] = result[n]


def attend(codes, first, keys, values, pick, bias, sources, cols, bases, out, chunk, heads, kv_head, width):
    slot_len, (row_len, span) = sources[0].shape[1], bias.shape
    chunk_width = heads * HEAD_DIM
    one_head = pl.BlockSpec((None, DOC_MAX + row_len, HEAD_DIM), lambda t, *_: (kv_head, 0, 0))
    operands = [codes, first, keys, values, pick, bias, *sources]
    specs = [one_head, one_head, WHOLE, WHOLE] + [ANYWHERE] * len(sources)
    aliases = {}
    if out is not None:
        aliases = {len(operands): 0}
        operands.append(out)
        specs.append(ANYWHERE)
    return pl.pallas_call(
        functools.partial(attend_kernel, cols=cols, bases=bases, heads=heads),
        grid_spec=pltpu.PrefetchScalarGridSpec(
            num_scalar_prefetch=2,
            grid=(row_len // TILE,),
            in_specs=specs,
            out_specs=pl.BlockSpec((TILE, chunk_width), lambda t, *_: (t, chunk)),
            scratch_shapes=[
                pltpu.VMEM((codes.shape[0], slot_len, chunk_width), jnp.bfloat16),
                pltpu.VMEM((heads * TILE, HEAD_DIM), jnp.bfloat16),
                pltpu.SemaphoreType.DMA,
            ],
        ),
        out_shape=jax.ShapeDtypeStruct((row_len, width), jnp.bfloat16),
        input_output_aliases=aliases,
        compiler_params=pltpu.CompilerParams(vmem_limit_bytes=32 << 20),
        cost_estimate=pl.CostEstimate(
            flops=4 * row_len * span * chunk_width,
            transcendentals=row_len * span * heads,
            bytes_accessed=6 * row_len * chunk_width,
        ),
        name="attend",
    )(*operands)


def flip(rows, bit):
    pairs = [(i, i ^ bit) for i in range(lax.axis_size("dp"))]
    return lax.ppermute(rows, "dp", pairs)


def lists_of(masks, codes, slots):
    items = masks.shape[1]
    upto = jnp.arange(items)[:, None] <= jnp.arange(items)[None, :]
    rank = jnp.dot(
        masks.astype(jnp.bfloat16), upto.astype(jnp.bfloat16), preferred_element_type=jnp.float32
    ).astype(jnp.int32) - 1
    rank = jnp.where(masks, rank, -1)
    if codes is None:
        return rank
    at = rank[:, None, :] == jnp.arange(slots, dtype=jnp.int32)[None, :, None]
    return jnp.sum(jnp.where(at, codes, 0), axis=2)


def hop_tables(dest, source, lane, me, groups, sentences, first_bit, second_bit):
    cross1 = ((dest ^ source) & first_bit) != 0
    place1 = jnp.where(cross1, source ^ first_bit, source)
    cross2 = ((dest ^ source) & second_bit) != 0
    place2 = jnp.where(cross2, place1 ^ second_bit, place1)
    cross3 = ((dest ^ source) & 1) != 0
    arrive = [
        (source == me ^ first_bit) & cross1,
        (place1 == me ^ second_bit) & cross2,
        (place2 == me ^ 1) & cross3,
    ]
    rank = lists_of(jnp.stack(arrive), None, None)
    away = source ^ me
    code = jnp.where(
        away == 0,
        lane,
        jnp.where(
            (away & 1) != 0,
            3 * sentences + rank[2],
            jnp.where((away & second_bit) != 0, 2 * sentences + rank[1], sentences + rank[0]),
        ),
    )
    send = [
        (source == me) & cross1,
        (place1 == me) & cross2,
        (place2 == me) & cross3,
        dest == me,
    ]
    lists = lists_of(jnp.stack(send), code[None, None, :], sentences)
    every = jnp.arange(groups, dtype=jnp.int32)[:, None]
    loads = [
        jnp.sum(((at[None, :] == every) & cross[None, :]).astype(jnp.int32), axis=1)
        for at, cross in ((source, cross1), (place1, cross2), (place2, cross3))
    ]
    return lists, jnp.max(jnp.stack(loads))


def journey(rows, col, width, lists, cap, bits, sentences):
    sources, cols = [rows], [col]
    bases = tuple(n * sentences for n in range(4))
    for hop, bit in enumerate((*bits, 1)):
        sent = gather(
            lists[hop, :cap], sources, tuple(cols), bases[: len(sources)], width
        )
        sources, cols = sources + [flip(sent, bit)], cols + [0]
    return sources, tuple(cols), bases


def per_device(queries, key_rows, value_rows, destination, token_count, doc_ids):
    groups = lax.axis_size("dp")
    ways = lax.axis_size("tensor")
    me = lax.axis_index("dp")
    sentences = destination.shape[0]
    slot_len = queries.shape[1]
    row_len = doc_ids.shape[1]
    q_width = queries.shape[2]
    kv_width = key_rows.shape[2] // ways
    kv_local = kv_width // HEAD_DIM
    per_group = q_width // kv_width
    heads = min(CHUNK_HEADS, per_group)
    chunk_width = heads * HEAD_DIM

    table = lax.all_gather(jnp.stack([destination, token_count]), "dp", axis=0)

    def split(rows):
        return rows.reshape(rows.shape[0], slot_len, ways, kv_width)

    kv = jnp.concatenate([split(key_rows), split(value_rows)], axis=3)
    kv = lax.all_to_all(
        jnp.transpose(kv, (2, 0, 1, 3)), "tensor", split_axis=0, concat_axis=0, tiled=True
    ).reshape(sentences, slot_len, 2 * kv_width)

    dest = table[:, 0, :].reshape(-1)
    counts = table[:, 1, :].reshape(-1)
    source = jnp.repeat(jnp.arange(groups, dtype=jnp.int32), sentences)
    lane = jnp.tile(jnp.arange(sentences, dtype=jnp.int32), groups)

    count_of = lists_of((dest == me)[None], counts[None, None, :], sentences)[0]
    nth = jnp.arange(sentences, dtype=jnp.int32)
    ends = jnp.sum(jnp.where(nth[None, :] <= nth[:, None], count_of[None, :], 0), axis=1)
    place = jnp.arange(row_len, dtype=jnp.int32)
    passed = place[:, None] >= ends[None, :]
    which = jnp.sum(passed.astype(jnp.int32), axis=1)
    start = jnp.sum(jnp.where(passed, count_of[None, :], 0), axis=1)
    live = which < sentences
    spread = min(sentences, (TILE - 1 + LEAST - 1) // LEAST + 1)
    heads_of = place[::TILE]
    first = jnp.sum((heads_of[:, None] >= ends[None, :]).astype(jnp.int32), axis=1)
    first = jnp.minimum(first, sentences - spread)
    window = spread * slot_len
    relative = (which - jnp.repeat(first, TILE)) * slot_len + place - start
    pick = (
        live[:, None] & (relative[:, None] == jnp.arange(window, dtype=jnp.int32)[None, :])
    ).astype(jnp.bfloat16)
    span = DOC_MAX + TILE
    padded = jnp.concatenate([jnp.full((DOC_MAX,), -1, jnp.int32), doc_ids[0]])
    tiles = row_len // TILE
    key_docs = jnp.stack([padded[t * TILE : t * TILE + span] for t in range(tiles)])
    col = jnp.arange(span, dtype=jnp.int32)[None, None, :]
    row = jnp.arange(TILE, dtype=jnp.int32)[None, :, None]
    allowed = (
        (col - DOC_MAX <= row)
        & (key_docs[:, None, :] == doc_ids[0].reshape(tiles, TILE)[:, :, None])
        & live.reshape(tiles, TILE)[:, :, None]
    )
    bias = jnp.where(allowed, 0.0, NEG).astype(jnp.float32).reshape(row_len, span)

    chunks = q_width // chunk_width

    def attend_all(got_kv, kv_codes, got_q, q_codes):
        keys, values = pack(kv_codes, first, pick, *got_kv, kv_local)
        out = None
        turn = sorted(range(chunks), key=lambda n: (n % (chunks // 2 or 1), n))
        for chunk in turn:
            kv_head = chunk * heads // per_group
            out = attend(
                q_codes[chunk], first, keys, values, pick, bias, *got_q[chunk], out, chunk, heads,
                kv_head, q_width,
            )
        return out

    if groups != 8:
        capacity = max(2, (2 * sentences + groups - 1) // groups)
        rank = lists_of(destination[None, :] == jnp.arange(groups, dtype=jnp.int32)[:, None], None, None)
        slot = jnp.arange(capacity, dtype=jnp.int32)
        at = rank[:, None, :] == slot[None, :, None]
        picked = jnp.sum(jnp.where(at, nth[None, None, :], 0), axis=2).reshape(-1)
        by_source = (dest == me).reshape(groups, sentences)
        rank_in = lists_of(by_source, None, None).reshape(-1)
        codes = lists_of(
            (dest == me)[None], (source * capacity + rank_in)[None, None, :], sentences
        )[0]

        def exchange(rows, col, width):
            sent = gather(picked, [rows], (col,), (0,), width)
            got = lax.all_to_all(sent, "dp", split_axis=0, concat_axis=0, tiled=True)
            return [got], (0,), (0,)

        got_kv = exchange(kv, 0, 2 * kv_width)
        got_q = [exchange(queries, n * chunk_width, chunk_width) for n in range(chunks)]
        return attend_all(got_kv, codes, got_q, [codes] * chunks)

    bits = ((2, 4), (4, 2))
    tables, loads = zip(
        *(hop_tables(dest, source, lane, me, groups, sentences, *pair) for pair in bits)
    )
    most = jnp.maximum(*loads)
    caps = sorted({min(sentences, n) for n in (20, 22, 25, sentences)})

    def with_cap(cap, queries, kv, *tables):
        got_q = []
        for n in range(chunks):
            half = n * 2 // chunks
            got_q.append(
                journey(queries, n * chunk_width, chunk_width, tables[half], cap, bits[half], sentences)
            )
        got_kv = journey(kv, 0, 2 * kv_width, tables[0], cap, bits[0], sentences)
        return attend_all(
            got_kv, tables[0][3], got_q, [tables[n * 2 // chunks][3] for n in range(chunks)]
        )

    tier = sum((most > cap).astype(jnp.int32) for cap in caps[:-1])
    return lax.switch(
        tier, [functools.partial(with_cap, cap) for cap in caps], queries, kv, *tables
    )


def solution(mesh):
    placed = (
        P("dp", None, "tensor"),
        P(("dp", "tensor"), None, None),
        P(("dp", "tensor"), None, None),
        P("dp"),
        P("dp"),
        P("dp", None),
    )
    return jax.shard_map(
        per_device, mesh=mesh, in_specs=placed, out_specs=P("dp", "tensor"), check_vma=False
    )
```

```python
import functools
import jax
import jax.numpy as jnp
from jax import lax
from jax.experimental import pallas as pl
from jax.experimental.pallas import tpu as pltpu
from jax.sharding import PartitionSpec as P

HEAD_DIM = 128
DOC_MAX = 256
LEAST = 16
TILE = 128
CHUNK_HEADS = 8
STACK = 4
NEG = -1e30
LOG2E = 1.4426950408889634
WHOLE = pl.BlockSpec(memory_space=pltpu.VMEM)
ANYWHERE = pl.BlockSpec(memory_space=pl.ANY)


def fetch(code_ref, sources, cols, bases, buf, sem):
    def one(k, carry):
        code = code_ref[k]
        for i, (source, col) in enumerate(zip(sources, cols)):

            def start(i=i, source=source, col=col):
                pltpu.make_async_copy(
                    source.at[code - bases[i], :, pl.ds(col, buf.shape[2])], buf.at[k], sem
                ).start()

            if len(sources) == 1:
                start()
            else:
                inside = code >= bases[i]
                if i + 1 < len(sources):
                    inside = inside & (code < bases[i + 1])
                pl.when(inside)(start)
        return carry

    lax.fori_loop(0, buf.shape[0], one, 0, unroll=4 if buf.shape[0] % 4 == 0 else 1)


def gather_kernel(code_ref, *rest, cols, bases):
    *sources, out_ref, sem = rest
    fetch(code_ref, sources, cols, bases, out_ref, sem)
    pltpu.make_async_copy(out_ref, out_ref, sem).wait()


def gather(codes, sources, cols, bases, width):
    slot_len = sources[0].shape[1]
    shape = (codes.shape[0], slot_len, width)
    return pl.pallas_call(
        functools.partial(gather_kernel, cols=cols, bases=bases),
        grid_spec=pltpu.PrefetchScalarGridSpec(
            num_scalar_prefetch=1,
            grid=(1,),
            in_specs=[ANYWHERE] * len(sources),
            out_specs=pl.BlockSpec(shape, lambda i, *_: (0, 0, 0)),
            scratch_shapes=[pltpu.SemaphoreType.DMA],
        ),
        out_shape=jax.ShapeDtypeStruct(shape, sources[0].dtype),
        compiler_params=pltpu.CompilerParams(vmem_limit_bytes=16 << 20),
        cost_estimate=pl.CostEstimate(
            flops=0, transcendentals=0, bytes_accessed=4 * shape[0] * slot_len * width
        ),
        name="gather",
    )(codes, *sources)


def pack_kernel(code_ref, first_ref, pick_ref, *rest, cols, bases):
    *sources, k_ref, v_ref, buf, sem = rest
    kv_local, slot_len, window = k_ref.shape[0], buf.shape[1], pick_ref.shape[1]
    fetch(code_ref, sources, cols, bases, buf, sem)
    pltpu.make_async_copy(buf, buf, sem).wait()
    for ref in (k_ref, v_ref):
        ref[:, :DOC_MAX, :] = jnp.zeros((kv_local, DOC_MAX, HEAD_DIM), jnp.bfloat16)

    @pl.loop(0, pick_ref.shape[0] // TILE)
    def _(t):
        here = pl.multiple_of(t * TILE, TILE)
        rows = buf[pl.ds(first_ref[t], window // slot_len)].reshape(window, buf.shape[2])
        packed = jnp.dot(
            pick_ref[pl.ds(here, TILE), :], rows, preferred_element_type=jnp.float32
        ).astype(jnp.bfloat16)
        for n in range(2 * kv_local):
            ref = (k_ref, v_ref)[n // kv_local]
            ref[n % kv_local, pl.ds(DOC_MAX + here, TILE), :] = packed[
                :, n * HEAD_DIM : (n + 1) * HEAD_DIM
            ]


def pack(codes, first, pick, sources, cols, bases, kv_local):
    slot_len = sources[0].shape[1]
    shape = jax.ShapeDtypeStruct((kv_local, DOC_MAX + pick.shape[0], HEAD_DIM), jnp.bfloat16)
    return pl.pallas_call(
        functools.partial(pack_kernel, cols=cols, bases=bases),
        grid_spec=pltpu.PrefetchScalarGridSpec(
            num_scalar_prefetch=2,
            grid=(1,),
            in_specs=[WHOLE] + [ANYWHERE] * len(sources),
            out_specs=[WHOLE, WHOLE],
            scratch_shapes=[
                pltpu.VMEM((codes.shape[0], slot_len, 2 * kv_local * HEAD_DIM), jnp.bfloat16),
                pltpu.SemaphoreType.DMA,
            ],
        ),
        out_shape=[shape, shape],
        compiler_params=pltpu.CompilerParams(vmem_limit_bytes=16 << 20),
        name="pack",
    )(codes, first, pick, *sources)


def attend_kernel(code_ref, first_ref, k_ref, v_ref, pick_ref, bias_ref, *rest, cols, bases, heads):
    *sources, out_ref, q_buf, q_rows, sem = rest
    sources = sources[: len(cols)]
    tile = pl.program_id(0)
    slot_len, window = q_buf.shape[1], pick_ref.shape[1]
    span = bias_ref.shape[1]

    @pl.when(tile == 0)
    def _():
        fetch(code_ref, sources, cols, bases, q_buf, sem)
        pltpu.make_async_copy(q_buf, q_buf, sem).wait()

    here = pl.multiple_of(tile * TILE, TILE)
    pick = pick_ref[pl.ds(here, TILE), :]
    bias = bias_ref[pl.ds(here, TILE), :]
    live = jnp.max(bias, axis=1, keepdims=True) > -1.0
    keys = k_ref[pl.ds(here, span), :]
    values = v_ref[pl.ds(here, span), :]
    rows = q_buf[pl.ds(first_ref[tile], window // slot_len)].reshape(window, q_buf.shape[2])
    packed = jnp.dot(pick, rows, preferred_element_type=jnp.float32).astype(jnp.bfloat16)
    for h in range(heads):
        q_rows[h * TILE : (h + 1) * TILE, :] = packed[:, h * HEAD_DIM : (h + 1) * HEAD_DIM]
    scale = (HEAD_DIM**-0.5) * LOG2E
    stack = min(STACK, heads)
    for g in range(heads // stack):
        score = lax.dot_general(
            q_rows[g * stack * TILE : (g + 1) * stack * TILE, :],
            keys,
            (((1,), (1,)), ((), ())),
            preferred_element_type=jnp.float32,
        ).reshape(stack, TILE, span)
        score = score * scale + bias[None]
        peak = jnp.max(score, axis=2, keepdims=True)
        weight = jnp.exp2(score - peak)
        norm = jnp.sum(weight, axis=2, keepdims=True)
        mixed = jnp.dot(
            weight.astype(jnp.bfloat16).reshape(stack * TILE, span),
            values,
            preferred_element_type=jnp.float32,
        ).reshape(stack, TILE, HEAD_DIM)
        result = jnp.where(live[None], mixed / norm, 0.0).astype(jnp.bfloat16)
        for n in range(stack):
            h = g * stack + n
            out_ref[:, h * HEAD_DIM : (h + 1) * HEAD_DIM] = result[n]


def attend(codes, first, keys, values, pick, bias, sources, cols, bases, out, chunk, heads, kv_head, width):
    slot_len, (row_len, span) = sources[0].shape[1], bias.shape
    chunk_width = heads * HEAD_DIM
    one_head = pl.BlockSpec((None, DOC_MAX + row_len, HEAD_DIM), lambda t, *_: (kv_head, 0, 0))
    operands = [codes, first, keys, values, pick, bias, *sources]
    specs = [one_head, one_head, WHOLE, WHOLE] + [ANYWHERE] * len(sources)
    aliases = {}
    if out is not None:
        aliases = {len(operands): 0}
        operands.append(out)
        specs.append(ANYWHERE)
    return pl.pallas_call(
        functools.partial(attend_kernel, cols=cols, bases=bases, heads=heads),
        grid_spec=pltpu.PrefetchScalarGridSpec(
            num_scalar_prefetch=2,
            grid=(row_len // TILE,),
            in_specs=specs,
            out_specs=pl.BlockSpec((TILE, chunk_width), lambda t, *_: (t, chunk)),
            scratch_shapes=[
                pltpu.VMEM((codes.shape[0], slot_len, chunk_width), jnp.bfloat16),
                pltpu.VMEM((heads * TILE, HEAD_DIM), jnp.bfloat16),
                pltpu.SemaphoreType.DMA,
            ],
        ),
        out_shape=jax.ShapeDtypeStruct((row_len, width), jnp.bfloat16),
        input_output_aliases=aliases,
        compiler_params=pltpu.CompilerParams(vmem_limit_bytes=32 << 20),
        cost_estimate=pl.CostEstimate(
            flops=4 * row_len * span * chunk_width,
            transcendentals=row_len * span * heads,
            bytes_accessed=6 * row_len * chunk_width,
        ),
        name="attend",
    )(*operands)


def flip(rows, bit):
    pairs = [(i, i ^ bit) for i in range(lax.axis_size("dp"))]
    return lax.ppermute(rows, "dp", pairs)


def lists_of(masks, codes, slots):
    items = masks.shape[1]
    upto = jnp.arange(items)[:, None] <= jnp.arange(items)[None, :]
    rank = jnp.dot(
        masks.astype(jnp.bfloat16), upto.astype(jnp.bfloat16), preferred_element_type=jnp.float32
    ).astype(jnp.int32) - 1
    rank = jnp.where(masks, rank, -1)
    if codes is None:
        return rank
    at = rank[:, None, :] == jnp.arange(slots, dtype=jnp.int32)[None, :, None]
    return jnp.sum(jnp.where(at, codes, 0), axis=2)


def hop_tables(dest, source, lane, me, groups, sentences, first_bit, second_bit):
    cross1 = ((dest ^ source) & first_bit) != 0
    place1 = jnp.where(cross1, source ^ first_bit, source)
    cross2 = ((dest ^ source) & second_bit) != 0
    place2 = jnp.where(cross2, place1 ^ second_bit, place1)
    cross3 = ((dest ^ source) & 1) != 0
    arrive = [
        (source == me ^ first_bit) & cross1,
        (place1 == me ^ second_bit) & cross2,
        (place2 == me ^ 1) & cross3,
    ]
    rank = lists_of(jnp.stack(arrive), None, None)
    away = source ^ me
    code = jnp.where(
        away == 0,
        lane,
        jnp.where(
            (away & 1) != 0,
            3 * sentences + rank[2],
            jnp.where((away & second_bit) != 0, 2 * sentences + rank[1], sentences + rank[0]),
        ),
    )
    send = [
        (source == me) & cross1,
        (place1 == me) & cross2,
        (place2 == me) & cross3,
        dest == me,
    ]
    lists = lists_of(jnp.stack(send), code[None, None, :], sentences)
    every = jnp.arange(groups, dtype=jnp.int32)[:, None]
    loads = [
        jnp.sum(((at[None, :] == every) & cross[None, :]).astype(jnp.int32), axis=1)
        for at, cross in ((source, cross1), (place1, cross2), (place2, cross3))
    ]
    return lists, jnp.max(jnp.stack(loads))


class Journey:
    def __init__(self, rows, col, width, lists, cap, bits, sentences):
        self.sources, self.cols, self.width = [rows], [col], width
        self.lists, self.cap, self.bits = lists, cap, (*bits, 1)
        self.bases = tuple(n * sentences for n in range(4))

    def collect(self):
        hop = len(self.sources) - 1
        self.sent = gather(
            self.lists[hop, : self.cap],
            self.sources,
            tuple(self.cols),
            self.bases[: hop + 1],
            self.width,
        )

    def hop(self):
        self.collect()
        self.travel()

    def travel(self):
        bit = self.bits[len(self.sources) - 1]
        self.sources = self.sources + [flip(self.sent, bit)]
        self.cols = self.cols + [0]

    def got(self):
        return self.sources, tuple(self.cols), self.bases


def per_device(queries, key_rows, value_rows, destination, token_count, doc_ids):
    groups = lax.axis_size("dp")
    ways = lax.axis_size("tensor")
    me = lax.axis_index("dp")
    sentences = destination.shape[0]
    slot_len = queries.shape[1]
    row_len = doc_ids.shape[1]
    q_width = queries.shape[2]
    kv_width = key_rows.shape[2] // ways
    kv_local = kv_width // HEAD_DIM
    per_group = q_width // kv_width
    heads = min(CHUNK_HEADS, per_group)
    chunk_width = heads * HEAD_DIM

    table = lax.all_gather(jnp.stack([destination, token_count]), "dp", axis=0)

    def split(rows):
        return rows.reshape(rows.shape[0], slot_len, ways, kv_width)

    def own_heads(key_rows, value_rows):
        kv = jnp.concatenate([split(key_rows), split(value_rows)], axis=3)
        return lax.all_to_all(
            jnp.transpose(kv, (2, 0, 1, 3)), "tensor", split_axis=0, concat_axis=0, tiled=True
        ).reshape(sentences, slot_len, 2 * kv_width)

    dest = table[:, 0, :].reshape(-1)
    counts = table[:, 1, :].reshape(-1)
    source = jnp.repeat(jnp.arange(groups, dtype=jnp.int32), sentences)
    lane = jnp.tile(jnp.arange(sentences, dtype=jnp.int32), groups)

    count_of = lists_of((dest == me)[None], counts[None, None, :], sentences)[0]
    nth = jnp.arange(sentences, dtype=jnp.int32)
    ends = jnp.sum(jnp.where(nth[None, :] <= nth[:, None], count_of[None, :], 0), axis=1)
    place = jnp.arange(row_len, dtype=jnp.int32)
    passed = place[:, None] >= ends[None, :]
    which = jnp.sum(passed.astype(jnp.int32), axis=1)
    start = jnp.sum(jnp.where(passed, count_of[None, :], 0), axis=1)
    live = which < sentences
    spread = min(sentences, (TILE - 1 + LEAST - 1) // LEAST + 1)
    heads_of = place[::TILE]
    first = jnp.sum((heads_of[:, None] >= ends[None, :]).astype(jnp.int32), axis=1)
    first = jnp.minimum(first, sentences - spread)
    window = spread * slot_len
    relative = (which - jnp.repeat(first, TILE)) * slot_len + place - start
    pick = (
        live[:, None] & (relative[:, None] == jnp.arange(window, dtype=jnp.int32)[None, :])
    ).astype(jnp.bfloat16)
    span = DOC_MAX + TILE
    padded = jnp.concatenate([jnp.full((DOC_MAX,), -1, jnp.int32), doc_ids[0]])
    tiles = row_len // TILE
    key_docs = jnp.stack([padded[t * TILE : t * TILE + span] for t in range(tiles)])
    col = jnp.arange(span, dtype=jnp.int32)[None, None, :]
    row = jnp.arange(TILE, dtype=jnp.int32)[None, :, None]
    allowed = (
        (col - DOC_MAX <= row)
        & (key_docs[:, None, :] == doc_ids[0].reshape(tiles, TILE)[:, :, None])
        & live.reshape(tiles, TILE)[:, :, None]
    )
    bias = jnp.where(allowed, 0.0, NEG).astype(jnp.float32).reshape(row_len, span)

    chunks = q_width // chunk_width

    def attend_one(chunk, kv_packed, first, got, codes, out):
        return attend(
            codes, first, *kv_packed, pick, bias, *got, out, chunk, heads, chunk * heads // per_group, q_width
        )

    if groups != 8:
        capacity = max(2, (2 * sentences + groups - 1) // groups)
        rank = lists_of(destination[None, :] == jnp.arange(groups, dtype=jnp.int32)[:, None], None, None)
        slot = jnp.arange(capacity, dtype=jnp.int32)
        at = rank[:, None, :] == slot[None, :, None]
        picked = jnp.sum(jnp.where(at, nth[None, None, :], 0), axis=2).reshape(-1)
        by_source = (dest == me).reshape(groups, sentences)
        rank_in = lists_of(by_source, None, None).reshape(-1)
        codes = lists_of(
            (dest == me)[None], (source * capacity + rank_in)[None, None, :], sentences
        )[0]

        def exchange(rows, col, width):
            sent = gather(picked, [rows], (col,), (0,), width)
            got = lax.all_to_all(sent, "dp", split_axis=0, concat_axis=0, tiled=True)
            return [got], (0,), (0,)

        got_kv = exchange(own_heads(key_rows, value_rows), 0, 2 * kv_width)
        got_q = [exchange(queries, n * chunk_width, chunk_width) for n in range(chunks)]
        kv_packed = pack(codes, first, pick, *got_kv, kv_local)
        out = None
        for n in range(chunks):
            out = attend_one(n, kv_packed, first, got_q[n], codes, out)
        return out

    bits = ((2, 4), (4, 2))
    tables, loads = zip(
        *(hop_tables(dest, source, lane, me, groups, sentences, *pair) for pair in bits)
    )
    most = jnp.maximum(*loads)
    caps = sorted({min(sentences, n) for n in (21, 23, 25, sentences)})

    def with_cap(cap, queries, key_rows, value_rows, *tables):
        halves = len(tables)

        def start(n, half):
            return Journey(
                queries, n * chunk_width, chunk_width, tables[half], cap, bits[half], sentences
            )

        per_half = chunks // halves
        rounds = [
            [start(half * per_half + n, half) for half in range(halves)] for n in range(per_half)
        ]
        for one in rounds[0]:
            one.hop()
        kv = Journey(
            own_heads(key_rows, value_rows), 0, 2 * kv_width, tables[0], cap, bits[0], sentences
        )
        kv.hop()
        ready = kv.sources[-1]
        flow_first, kv_packed, out = first, None, None
        for n in range(per_half):
            following = rounds[n + 1] if n + 1 < per_half else []
            if following:
                ready, *held = lax.optimization_barrier(
                    (ready, *(one.lists for one in following))
                )
                if n == 0:
                    kv.sources[-1] = ready
                for one, lists in zip(following, held):
                    one.lists = lists
                    one.hop()
            for one in rounds[n]:
                if n == 0:
                    one.hop()
            if n == 0:
                kv.hop()
            for one in rounds[n]:
                one.hop()
            if n == 0:
                kv.hop()
            if following:
                for one in following:
                    one.collect()
                flow_first, *sent = lax.optimization_barrier(
                    (first, *(one.sent for one in following))
                )
                for one, rows in zip(following, sent):
                    one.sent = rows
                    one.travel()
            if n == 0:
                kv_packed = pack(tables[0][3], flow_first, pick, *kv.got(), kv_local)
            for half, one in enumerate(rounds[n]):
                out = attend_one(
                    half * per_half + n, kv_packed, flow_first, one.got(), tables[half][3], out
                )
            if following:
                out, *held = lax.optimization_barrier((out, *(one.lists for one in following)))
                for one, lists in zip(following, held):
                    one.lists = lists
                ready, flow_first = out, first
        return out

    tier = sum((most > cap).astype(jnp.int32) for cap in caps[:-1])
    return lax.switch(
        tier, [functools.partial(with_cap, cap) for cap in caps], queries, key_rows, value_rows, *tables
    )


def solution(mesh):
    placed = (
        P("dp", None, "tensor"),
        P(("dp", "tensor"), None, None),
        P(("dp", "tensor"), None, None),
        P("dp"),
        P("dp"),
        P("dp", None),
    )
    return jax.shard_map(
        per_device, mesh=mesh, in_specs=placed, out_specs=P("dp", "tensor"), check_vma=False
    )
```

```python
import functools
import jax
import jax.numpy as jnp
from jax import lax
from jax.experimental import pallas as pl
from jax.experimental.pallas import tpu as pltpu
from jax.sharding import PartitionSpec as P

HEAD_DIM = 128
DOC_MAX = 256
LEAST = 16
TILE = 128
CHUNK_HEADS = 8
STACK = 4
NEG = -1e30
LOG2E = 1.4426950408889634
WHOLE = pl.BlockSpec(memory_space=pltpu.VMEM)
ANYWHERE = pl.BlockSpec(memory_space=pl.ANY)


def fetch(code_ref, sources, cols, bases, buf, sem):
    def one(k, carry):
        code = code_ref[k]
        for i, (source, col) in enumerate(zip(sources, cols)):

            def start(i=i, source=source, col=col):
                pltpu.make_async_copy(
                    source.at[code - bases[i], :, pl.ds(col, buf.shape[2])], buf.at[k], sem
                ).start()

            if len(sources) == 1:
                start()
            else:
                inside = code >= bases[i]
                if i + 1 < len(sources):
                    inside = inside & (code < bases[i + 1])
                pl.when(inside)(start)
        return carry

    lax.fori_loop(0, buf.shape[0], one, 0, unroll=4 if buf.shape[0] % 4 == 0 else 1)


def gather_kernel(code_ref, *rest, cols, bases):
    *sources, out_ref, sem = rest
    fetch(code_ref, sources, cols, bases, out_ref, sem)
    pltpu.make_async_copy(out_ref, out_ref, sem).wait()


def gather(codes, sources, cols, bases, width):
    slot_len = sources[0].shape[1]
    shape = (codes.shape[0], slot_len, width)
    return pl.pallas_call(
        functools.partial(gather_kernel, cols=cols, bases=bases),
        grid_spec=pltpu.PrefetchScalarGridSpec(
            num_scalar_prefetch=1,
            grid=(1,),
            in_specs=[ANYWHERE] * len(sources),
            out_specs=pl.BlockSpec(shape, lambda i, *_: (0, 0, 0)),
            scratch_shapes=[pltpu.SemaphoreType.DMA],
        ),
        out_shape=jax.ShapeDtypeStruct(shape, sources[0].dtype),
        compiler_params=pltpu.CompilerParams(vmem_limit_bytes=16 << 20),
        cost_estimate=pl.CostEstimate(
            flops=0, transcendentals=0, bytes_accessed=4 * shape[0] * slot_len * width
        ),
        name="gather",
    )(codes, *sources)


def pack_kernel(code_ref, first_ref, pick_ref, *rest, cols, bases):
    *sources, k_ref, v_ref, buf, sem = rest
    kv_local, slot_len, window = k_ref.shape[0], buf.shape[1], pick_ref.shape[1]
    fetch(code_ref, sources, cols, bases, buf, sem)
    pltpu.make_async_copy(buf, buf, sem).wait()
    for ref in (k_ref, v_ref):
        ref[:, :DOC_MAX, :] = jnp.zeros((kv_local, DOC_MAX, HEAD_DIM), jnp.bfloat16)

    @pl.loop(0, pick_ref.shape[0] // TILE)
    def _(t):
        here = pl.multiple_of(t * TILE, TILE)
        rows = buf[pl.ds(first_ref[t], window // slot_len)].reshape(window, buf.shape[2])
        packed = jnp.dot(
            pick_ref[pl.ds(here, TILE), :], rows, preferred_element_type=jnp.float32
        ).astype(jnp.bfloat16)
        for n in range(2 * kv_local):
            ref = (k_ref, v_ref)[n // kv_local]
            ref[n % kv_local, pl.ds(DOC_MAX + here, TILE), :] = packed[
                :, n * HEAD_DIM : (n + 1) * HEAD_DIM
            ]


def pack(codes, first, pick, sources, cols, bases, kv_local):
    slot_len = sources[0].shape[1]
    shape = jax.ShapeDtypeStruct((kv_local, DOC_MAX + pick.shape[0], HEAD_DIM), jnp.bfloat16)
    return pl.pallas_call(
        functools.partial(pack_kernel, cols=cols, bases=bases),
        grid_spec=pltpu.PrefetchScalarGridSpec(
            num_scalar_prefetch=2,
            grid=(1,),
            in_specs=[WHOLE] + [ANYWHERE] * len(sources),
            out_specs=[WHOLE, WHOLE],
            scratch_shapes=[
                pltpu.VMEM((codes.shape[0], slot_len, 2 * kv_local * HEAD_DIM), jnp.bfloat16),
                pltpu.SemaphoreType.DMA,
            ],
        ),
        out_shape=[shape, shape],
        compiler_params=pltpu.CompilerParams(vmem_limit_bytes=16 << 20),
        name="pack",
    )(codes, first, pick, *sources)


def attend_kernel(code_ref, first_ref, k_ref, v_ref, pick_ref, bias_ref, *rest, cols, bases, heads):
    *sources, out_ref, q_buf, q_rows, sem = rest
    sources = sources[: len(cols)]
    tile = pl.program_id(0)
    slot_len, window = q_buf.shape[1], pick_ref.shape[1]
    span = bias_ref.shape[1]

    @pl.when(tile == 0)
    def _():
        fetch(code_ref, sources, cols, bases, q_buf, sem)
        pltpu.make_async_copy(q_buf, q_buf, sem).wait()

    here = pl.multiple_of(tile * TILE, TILE)
    pick = pick_ref[pl.ds(here, TILE), :]
    bias = bias_ref[pl.ds(here, TILE), :]
    live = jnp.max(bias, axis=1, keepdims=True) > -1.0
    keys = k_ref[pl.ds(here, span), :]
    values = v_ref[pl.ds(here, span), :]
    rows = q_buf[pl.ds(first_ref[tile], window // slot_len)].reshape(window, q_buf.shape[2])
    packed = jnp.dot(pick, rows, preferred_element_type=jnp.float32).astype(jnp.bfloat16)
    for h in range(heads):
        q_rows[h * TILE : (h + 1) * TILE, :] = packed[:, h * HEAD_DIM : (h + 1) * HEAD_DIM]
    scale = (HEAD_DIM**-0.5) * LOG2E
    stack = min(STACK, heads)
    for g in range(heads // stack):
        score = lax.dot_general(
            q_rows[g * stack * TILE : (g + 1) * stack * TILE, :],
            keys,
            (((1,), (1,)), ((), ())),
            preferred_element_type=jnp.float32,
        ).reshape(stack, TILE, span)
        score = score * scale + bias[None]
        peak = jnp.max(score, axis=2, keepdims=True)
        weight = jnp.exp2(score - peak)
        norm = jnp.sum(weight, axis=2, keepdims=True)
        mixed = jnp.dot(
            weight.astype(jnp.bfloat16).reshape(stack * TILE, span),
            values,
            preferred_element_type=jnp.float32,
        ).reshape(stack, TILE, HEAD_DIM)
        result = jnp.where(live[None], mixed / norm, 0.0).astype(jnp.bfloat16)
        for n in range(stack):
            h = g * stack + n
            out_ref[:, h * HEAD_DIM : (h + 1) * HEAD_DIM] = result[n]


def attend(codes, first, keys, values, pick, bias, sources, cols, bases, out, chunk, heads, kv_head, width):
    slot_len, (row_len, span) = sources[0].shape[1], bias.shape
    chunk_width = heads * HEAD_DIM
    one_head = pl.BlockSpec((None, DOC_MAX + row_len, HEAD_DIM), lambda t, *_: (kv_head, 0, 0))
    operands = [codes, first, keys, values, pick, bias, *sources]
    specs = [one_head, one_head, WHOLE, WHOLE] + [ANYWHERE] * len(sources)
    aliases = {}
    if out is not None:
        aliases = {len(operands): 0}
        operands.append(out)
        specs.append(ANYWHERE)
    return pl.pallas_call(
        functools.partial(attend_kernel, cols=cols, bases=bases, heads=heads),
        grid_spec=pltpu.PrefetchScalarGridSpec(
            num_scalar_prefetch=2,
            grid=(row_len // TILE,),
            in_specs=specs,
            out_specs=pl.BlockSpec((TILE, chunk_width), lambda t, *_: (t, chunk)),
            scratch_shapes=[
                pltpu.VMEM((codes.shape[0], slot_len, chunk_width), jnp.bfloat16),
                pltpu.VMEM((heads * TILE, HEAD_DIM), jnp.bfloat16),
                pltpu.SemaphoreType.DMA,
            ],
        ),
        out_shape=jax.ShapeDtypeStruct((row_len, width), jnp.bfloat16),
        input_output_aliases=aliases,
        compiler_params=pltpu.CompilerParams(vmem_limit_bytes=32 << 20),
        cost_estimate=pl.CostEstimate(
            flops=4 * row_len * span * chunk_width,
            transcendentals=row_len * span * heads,
            bytes_accessed=6 * row_len * chunk_width,
        ),
        name="attend",
    )(*operands)


def flip(rows, bit):
    pairs = [(i, i ^ bit) for i in range(lax.axis_size("dp"))]
    return lax.ppermute(rows, "dp", pairs)


def lists_of(masks, codes, slots):
    items = masks.shape[1]
    upto = jnp.arange(items)[:, None] <= jnp.arange(items)[None, :]
    rank = jnp.dot(
        masks.astype(jnp.bfloat16), upto.astype(jnp.bfloat16), preferred_element_type=jnp.float32
    ).astype(jnp.int32) - 1
    rank = jnp.where(masks, rank, -1)
    if codes is None:
        return rank
    at = rank[:, None, :] == jnp.arange(slots, dtype=jnp.int32)[None, :, None]
    return jnp.sum(jnp.where(at, codes, 0), axis=2)


def hop_tables(dest, source, lane, me, groups, sentences, first_bit, second_bit):
    cross1 = ((dest ^ source) & first_bit) != 0
    place1 = jnp.where(cross1, source ^ first_bit, source)
    cross2 = ((dest ^ source) & second_bit) != 0
    place2 = jnp.where(cross2, place1 ^ second_bit, place1)
    cross3 = ((dest ^ source) & 1) != 0
    arrive = [
        (source == me ^ first_bit) & cross1,
        (place1 == me ^ second_bit) & cross2,
        (place2 == me ^ 1) & cross3,
    ]
    rank = lists_of(jnp.stack(arrive), None, None)
    away = source ^ me
    code = jnp.where(
        away == 0,
        lane,
        jnp.where(
            (away & 1) != 0,
            3 * sentences + rank[2],
            jnp.where((away & second_bit) != 0, 2 * sentences + rank[1], sentences + rank[0]),
        ),
    )
    send = [
        (source == me) & cross1,
        (place1 == me) & cross2,
        (place2 == me) & cross3,
        dest == me,
    ]
    lists = lists_of(jnp.stack(send), code[None, None, :], sentences)
    every = jnp.arange(groups, dtype=jnp.int32)[:, None]
    loads = [
        jnp.sum(((at[None, :] == every) & cross[None, :]).astype(jnp.int32), axis=1)
        for at, cross in ((source, cross1), (place1, cross2), (place2, cross3))
    ]
    return lists, jnp.max(jnp.stack(loads))


class Journey:
    def __init__(self, rows, col, width, lists, cap, bits, sentences):
        self.sources, self.cols, self.width = [rows], [col], width
        self.lists, self.cap, self.bits = lists, cap, (*bits, 1)
        self.bases = tuple(n * sentences for n in range(4))

    def collect(self):
        hop = len(self.sources) - 1
        self.sent = gather(
            self.lists[hop, : self.cap],
            self.sources,
            tuple(self.cols),
            self.bases[: hop + 1],
            self.width,
        )

    def hop(self):
        self.collect()
        self.travel()

    def travel(self):
        bit = self.bits[len(self.sources) - 1]
        self.sources = self.sources + [flip(self.sent, bit)]
        self.cols = self.cols + [0]

    def got(self):
        return self.sources, tuple(self.cols), self.bases


def per_device(queries, key_rows, value_rows, destination, token_count, doc_ids):
    groups = lax.axis_size("dp")
    ways = lax.axis_size("tensor")
    me = lax.axis_index("dp")
    sentences = destination.shape[0]
    slot_len = queries.shape[1]
    row_len = doc_ids.shape[1]
    q_width = queries.shape[2]
    kv_width = key_rows.shape[2] // ways
    kv_local = kv_width // HEAD_DIM
    per_group = q_width // kv_width
    heads = min(CHUNK_HEADS, per_group)
    chunk_width = heads * HEAD_DIM

    table = lax.all_gather(jnp.stack([destination, token_count]), "dp", axis=0)

    def split(rows):
        return rows.reshape(rows.shape[0], slot_len, ways, kv_width)

    def own_heads(key_rows, value_rows):
        kv = jnp.concatenate([split(key_rows), split(value_rows)], axis=3)
        return lax.all_to_all(
            jnp.transpose(kv, (2, 0, 1, 3)), "tensor", split_axis=0, concat_axis=0, tiled=True
        ).reshape(sentences, slot_len, 2 * kv_width)

    dest = table[:, 0, :].reshape(-1)
    counts = table[:, 1, :].reshape(-1)
    source = jnp.repeat(jnp.arange(groups, dtype=jnp.int32), sentences)
    lane = jnp.tile(jnp.arange(sentences, dtype=jnp.int32), groups)

    count_of = lists_of((dest == me)[None], counts[None, None, :], sentences)[0]
    nth = jnp.arange(sentences, dtype=jnp.int32)
    ends = jnp.sum(jnp.where(nth[None, :] <= nth[:, None], count_of[None, :], 0), axis=1)
    place = jnp.arange(row_len, dtype=jnp.int32)
    passed = place[:, None] >= ends[None, :]
    which = jnp.sum(passed.astype(jnp.int32), axis=1)
    start = jnp.sum(jnp.where(passed, count_of[None, :], 0), axis=1)
    live = which < sentences
    spread = min(sentences, (TILE - 1 + LEAST - 1) // LEAST + 1)
    heads_of = place[::TILE]
    first = jnp.sum((heads_of[:, None] >= ends[None, :]).astype(jnp.int32), axis=1)
    first = jnp.minimum(first, sentences - spread)
    window = spread * slot_len
    relative = (which - jnp.repeat(first, TILE)) * slot_len + place - start
    pick = (
        live[:, None] & (relative[:, None] == jnp.arange(window, dtype=jnp.int32)[None, :])
    ).astype(jnp.bfloat16)
    span = DOC_MAX + TILE
    padded = jnp.concatenate([jnp.full((DOC_MAX,), -1, jnp.int32), doc_ids[0]])
    tiles = row_len // TILE
    key_docs = jnp.stack([padded[t * TILE : t * TILE + span] for t in range(tiles)])
    col = jnp.arange(span, dtype=jnp.int32)[None, None, :]
    row = jnp.arange(TILE, dtype=jnp.int32)[None, :, None]
    allowed = (
        (col - DOC_MAX <= row)
        & (key_docs[:, None, :] == doc_ids[0].reshape(tiles, TILE)[:, :, None])
        & live.reshape(tiles, TILE)[:, :, None]
    )
    bias = jnp.where(allowed, 0.0, NEG).astype(jnp.float32).reshape(row_len, span)

    chunks = q_width // chunk_width

    def attend_one(chunk, kv_packed, first, got, codes, out):
        return attend(
            codes, first, *kv_packed, pick, bias, *got, out, chunk, heads, chunk * heads // per_group, q_width
        )

    if groups != 8:
        capacity = max(2, (2 * sentences + groups - 1) // groups)
        rank = lists_of(destination[None, :] == jnp.arange(groups, dtype=jnp.int32)[:, None], None, None)
        slot = jnp.arange(capacity, dtype=jnp.int32)
        at = rank[:, None, :] == slot[None, :, None]
        picked = jnp.sum(jnp.where(at, nth[None, None, :], 0), axis=2).reshape(-1)
        by_source = (dest == me).reshape(groups, sentences)
        rank_in = lists_of(by_source, None, None).reshape(-1)
        codes = lists_of(
            (dest == me)[None], (source * capacity + rank_in)[None, None, :], sentences
        )[0]

        def exchange(rows, col, width):
            sent = gather(picked, [rows], (col,), (0,), width)
            got = lax.all_to_all(sent, "dp", split_axis=0, concat_axis=0, tiled=True)
            return [got], (0,), (0,)

        got_kv = exchange(own_heads(key_rows, value_rows), 0, 2 * kv_width)
        got_q = [exchange(queries, n * chunk_width, chunk_width) for n in range(chunks)]
        kv_packed = pack(codes, first, pick, *got_kv, kv_local)
        out = None
        for n in range(chunks):
            out = attend_one(n, kv_packed, first, got_q[n], codes, out)
        return out

    bits = ((2, 4), (4, 2))
    tables, loads = zip(
        *(hop_tables(dest, source, lane, me, groups, sentences, *pair) for pair in bits)
    )
    most = jnp.maximum(*loads)
    caps = sorted({min(sentences, n) for n in (21, 23, 25, sentences)})

    def with_cap(cap, queries, key_rows, value_rows, *tables):
        halves = len(tables)

        def start(n, half):
            return Journey(
                queries, n * chunk_width, chunk_width, tables[half], cap, bits[half], sentences
            )

        per_half = chunks // halves
        rounds = [
            [start(half * per_half + n, half) for half in range(halves)] for n in range(per_half)
        ]
        for one in rounds[0]:
            one.hop()
        kv = Journey(
            own_heads(key_rows, value_rows), 0, 2 * kv_width, tables[0], cap, bits[0], sentences
        )
        kv.hop()
        ready = kv.sources[-1]
        flow_first, kv_packed, out = first, None, None
        for n in range(per_half):
            following = rounds[n + 1] if n + 1 < per_half else []
            if following:
                ready, *held = lax.optimization_barrier(
                    (ready, *(one.lists for one in following))
                )
                if n == 0:
                    kv.sources[-1] = ready
                for one, lists in zip(following, held):
                    one.lists = lists
                    one.hop()
            for one in rounds[n]:
                if n == 0:
                    one.hop()
            if n == 0:
                kv.hop()
            for one in rounds[n]:
                one.hop()
            if n == 0:
                kv.hop()
            if n == 0:
                kv_packed = pack(tables[0][3], first, pick, *kv.got(), kv_local)
            for half, one in enumerate(rounds[n]):
                out = attend_one(
                    half * per_half + n, kv_packed, flow_first, one.got(), tables[half][3], out
                )
                if following and half == 0:
                    out, *held = lax.optimization_barrier((out, *(each.lists for each in following)))
                    for each, lists in zip(following, held):
                        each.lists = lists
                        each.collect()
                    flow_first, *sent = lax.optimization_barrier(
                        (first, *(each.sent for each in following))
                    )
                    for each, rows in zip(following, sent):
                        each.sent = rows
                        each.travel()
            if following:
                out, *held = lax.optimization_barrier((out, *(one.lists for one in following)))
                for one, lists in zip(following, held):
                    one.lists = lists
                ready, flow_first = out, first
        return out

    tier = sum((most > cap).astype(jnp.int32) for cap in caps[:-1])
    return lax.switch(
        tier, [functools.partial(with_cap, cap) for cap in caps], queries, key_rows, value_rows, *tables
    )


def solution(mesh):
    placed = (
        P("dp", None, "tensor"),
        P(("dp", "tensor"), None, None),
        P(("dp", "tensor"), None, None),
        P("dp"),
        P("dp"),
        P("dp", None),
    )
    return jax.shard_map(
        per_device, mesh=mesh, in_specs=placed, out_specs=P("dp", "tensor"), check_vma=False
    )
```
